32 devices in a mesh: gy: 4 (over y, x), gz: 8 (over z, core).
Axes of the slice: x: 2, y: 2, z: 4, core: 2. Of those that a mesh axis runs over, the one named last changes fastest.
Arguments:
- volume: float32 [128, 512, 128], P('gy', 'gz'), may hold values from -60 to 60
- cotangent: float32 [128, 512, 128], P('gy', 'gz'), may hold values from -96 to 96
Outputs:
- volume_grad: float32 [128, 512, 128], P('gy', 'gz')
The draws below stay inside these ranges and needn't reach their ends.
All inputs are finite; a program needn't handle non-finite values.
Results may differ from the reference program's by a relative error of at most 0.0045.
Values sent between devices are 32-bit elements; how exact they have to be, the bound alone decides.
A program may use at most 128 MiB of HBM per device.

```python
import math
import jax
import jax.numpy as jnp
import numpy as np
from jax import lax

NX = 128
CY = 32
CZ = 64
NY = 128
NZ = 512


def draw_cotangent(key, part):
    key_noise = jax.random.fold_in(key, 11)
    key_rowpart = jax.random.fold_in(key, 12)
    key_planepart = jax.random.fold_in(key, 13)
    row_ids = jnp.arange(NY, dtype=jnp.int32).reshape(NY, 1, 1)
    plane_ids = jnp.arange(NZ, dtype=jnp.int32).reshape(1, NZ, 1)
    row_local = row_ids % CY
    plane_local = plane_ids % CZ
    near_row = (jnp.minimum(row_local, CY - 1 - row_local) < 6).astype(jnp.float32)
    near_plane = (jnp.minimum(plane_local, CZ - 1 - plane_local) < 6).astype(jnp.float32)
    row_sign = (1 - 2 * (row_ids % 2)).astype(jnp.float32)
    plane_sign = (1 - 2 * (plane_ids % 2)).astype(jnp.float32)
    noise = jnp.clip(jax.random.normal(key_noise, (NY, NZ, NX), jnp.float32), -3.0, 3.0)
    row_common = jnp.clip(jax.random.normal(key_rowpart, (1, NZ, NX), jnp.float32), -3.0, 3.0)
    plane_common = jnp.clip(jax.random.normal(key_planepart, (NY, 1, NX), jnp.float32), -3.0, 3.0)
    value = 3.0 * noise + 12.0 * near_row * row_sign * row_common + 12.0 * near_plane * plane_sign * plane_common
    return value.astype(jnp.float32)


def block_scale(key, dims, pieces, smallest, top_value):
    gain = 1.0
    for position, parts in pieces:
        draws = jax.random.uniform(jax.random.fold_in(jax.random.fold_in(key, 6), position), (parts,), jnp.float32, smallest / len(pieces), top_value / len(pieces))
        gain = gain * jnp.repeat(jnp.exp(draws), dims[position] // parts).reshape((-1,) + (1,) * (len(dims) - 1 - position))
    return gain


def scatter_about(rng, dims, scale, most, cuts=(), kind=jnp.bfloat16):
    drawn = jax.random.normal(rng, dims, jnp.float32) * scale
    if len(cuts) > 0:
        drawn = block_scale(rng, dims, cuts, -0.22, 0.18) * drawn
    return jnp.clip(drawn, min=-most, max=most).astype(kind)


def setup_inputs(seed: int = 0) -> dict:
    seeds = jax.random.split(jax.random.key(seed), 3)
    volume = scatter_about(seeds[0], (NY, NZ, NX), 10.0, 60.0, ((0, 4), (1, 8)), jnp.float32)
    cotangent = draw_cotangent(jax.random.fold_in(seeds[2], 71), 0)
    return dict(volume=volume, cotangent=cotangent)


sigma_sq = 4.0
x_orders = [2, 0, 0, 1, 1, 0]
y_orders = [0, 2, 0, 1, 0, 1]
z_orders = [0, 0, 2, 0, 1, 1]

def kernel_taps(order, flipped):
    base = [math.exp(-offset * offset / 8.0) for offset in range(-6, 7)]
    total = sum(base)
    gauss = [value / total for value in base]
    if order == 0:
        taps = gauss
    elif order == 1:
        taps = [-(offset / 4.0) * gauss[offset + 6] for offset in range(-6, 7)]
    else:
        taps = [(offset * offset / 16.0 - 0.25) * gauss[offset + 6] for offset in range(-6, 7)]
    if flipped:
        taps = taps[::-1]
    return taps

def band_matrix(order, width):
    taps = kernel_taps(order, False)
    matrix = np.zeros((width, width))
    for shift_by in range(-6, 7):
        matrix = matrix + taps[6 - shift_by] * np.eye(width, k=shift_by)
    return jnp.asarray(matrix, jnp.float32)

def slide(field, taps, axis, length):
    accum = taps[0] * lax.slice_in_dim(field, 0, length, axis=axis)
    for offset in range(1, 13):
        accum = accum + taps[offset] * lax.slice_in_dim(field, offset, offset + length, axis=axis)
    return accum

def z_passes(extended, planes):
    return jnp.stack([slide(extended, kernel_taps(order, False), 1, planes) for order in range(3)])

def forward_rows(along_z, rows, width):
    members = []
    for member in range(6):
        field = slide(along_z[z_orders[member]], kernel_taps(y_orders[member], False), 0, rows)
        field = sigma_sq * jnp.dot(field, band_matrix(x_orders[member], width), precision=lax.Precision.HIGHEST)
        members.append(field)
    return jnp.stack(members)

def back_x(grads, width):
    members = []
    for member in range(6):
        matrix = band_matrix(x_orders[member], width)
        members.append(sigma_sq * jnp.dot(grads[member], matrix.T, precision=lax.Precision.HIGHEST))
    return jnp.stack(members)

def transposed_group(stack, axis, pass_orders, group_orders, length):
    groups = [None, None, None]
    for member in range(6):
        partial_value = slide(stack[member], kernel_taps(pass_orders[member], True), axis, length)
        bucket = group_orders[member]
        groups[bucket] = partial_value if groups[bucket] is None else groups[bucket] + partial_value
    return jnp.stack(groups)

def transposed_final(stack, axis, length):
    result = slide(stack[0], kernel_taps(0, True), axis, length)
    for order in range(1, 3):
        result = result + slide(stack[order], kernel_taps(order, True), axis, length)
    return result

def vessel_field(comps):
    h_xx, h_yy, h_zz = (comps[0], comps[1], comps[2])
    h_xy, h_xz, h_yz = (comps[3], comps[4], comps[5])
    mean_diag = (h_xx + h_yy + h_zz) / 3.0
    dev_xx = h_xx - mean_diag
    dev_yy = h_yy - mean_diag
    dev_zz = h_zz - mean_diag
    spread_sq = dev_xx * dev_xx + dev_yy * dev_yy + dev_zz * dev_zz + 2.0 * (h_xy * h_xy + h_xz * h_xz + h_yz * h_yz)
    radius = jnp.sqrt(spread_sq / 6.0)
    determ = dev_xx * (dev_yy * dev_zz - h_yz * h_yz) - h_xy * (h_xy * dev_zz - h_yz * h_xz) + h_xz * (h_xy * h_yz - dev_yy * h_xz)
    cosine = jnp.clip(determ / (2.0 * radius * radius * radius), -0.999999, 0.999999)
    third = jnp.arccos(cosine) / 3.0
    upper = mean_diag + 2.0 * radius * jnp.cos(third)
    lower = mean_diag + 2.0 * radius * jnp.cos(third + 2.0 * math.pi / 3.0)
    middle = 3.0 * mean_diag - upper - lower
    ratio_a = middle * middle / (lower * lower + 1.0)
    ratio_b = upper * upper / jnp.sqrt(middle * middle * lower * lower + 1.0)
    strength = upper * upper + middle * middle + lower * lower
    return (1.0 - jnp.exp(-2.0 * ratio_a)) * jnp.exp(-2.0 * ratio_b) * (1.0 - jnp.exp(-strength / 2.0))

def vessel_grad(comps, cotangent):
    value, pullback = jax.vjp(vessel_field, comps)
    return pullback(cotangent)[0]

def reference(volume, cotangent):
    rows, planes, width = volume.shape
    extended = jnp.pad(volume, ((6, 6), (6, 6), (0, 0)))
    along_z = z_passes(extended, planes)
    comps = forward_rows(along_z, rows, width)
    grads = lax.map(lambda bundle: vessel_grad(bundle[0], bundle[1]), (jnp.moveaxis(comps, 1, 0), cotangent))
    grads = jnp.moveaxis(grads, 0, 1)
    back_comps = back_x(grads, width)
    padded = jnp.pad(back_comps, ((0, 0), (6, 6), (0, 0), (0, 0)))
    groups = transposed_group(padded, 0, y_orders, z_orders, rows)
    groups = jnp.pad(groups, ((0, 0), (0, 0), (6, 6), (0, 0)))
    return transposed_final(groups, 1, planes)
```

```python
import functools
import math

import jax
import jax.numpy as jnp
import numpy as np
from jax import lax
from jax.experimental import pallas as pl
from jax.experimental.pallas import tpu as pltpu
from jax.sharding import PartitionSpec as P

REACH = 6
PAD = 8
X_ORDERS = (2, 0, 0, 1, 1, 0)
SIDES = [(dy, dz) for dy in (-1, 0, 1) for dz in (-1, 0, 1) if (dy, dz) != (0, 0)]


def kernel_taps(order):
    base = [math.exp(-t * t / 8.0) for t in range(-REACH, REACH + 1)]
    total = sum(base)
    scale = (
        lambda t: 1.0,
        lambda t: -(t / 4.0),
        lambda t: t * t / 16.0 - 0.25,
    )[order]
    return [scale(t) * base[t + REACH] / total for t in range(-REACH, REACH + 1)]


TAPS = [kernel_taps(order)[REACH:] for order in range(3)]


def split_weights(width):
    stacks = []
    for flip in (False, True):
        for order in range(3):
            taps = kernel_taps(order)
            band = np.zeros((width, width))
            for shift in range(-REACH, REACH + 1):
                band = band + taps[REACH - shift] * np.eye(width, k=shift)
            rest = 4.0 * (band.T if flip else band)
            parts = []
            for _ in range(3):
                parts.append(rest.astype(jnp.bfloat16))
                rest = rest - parts[-1].astype(np.float64)
            b1, b2, b3 = parts
            top = np.concatenate([b1, b2, b3], axis=1)
            bottom = np.concatenate([b1, b2, b1], axis=1)
            stacks.append(np.concatenate([top, bottom], axis=0))
    return np.stack(stacks)


def spread_weights(planes):
    deep = planes + 2 * PAD
    band = np.zeros((deep, 3 * planes))
    for order in range(3):
        taps = kernel_taps(order)
        for t in range(-REACH, REACH + 1):
            band[:, order * planes : (order + 1) * planes] += taps[t + REACH] * np.eye(
                deep, planes, k=-PAD - t
            )
    high = band.astype(jnp.bfloat16)
    low = (band - high.astype(np.float64)).astype(jnp.bfloat16)
    return np.concatenate([high, low], axis=0)


def even(values, order):
    taps = TAPS[order]
    out = taps[0] * values[REACH]
    for t in range(1, REACH + 1):
        out = out + taps[t] * (values[REACH + t] + values[REACH - t])
    return out


def odd(values):
    taps = TAPS[1]
    out = taps[1] * (values[REACH + 1] - values[REACH - 1])
    for t in range(2, REACH + 1):
        out = out + taps[t] * (values[REACH + t] - values[REACH - t])
    return out


def passes(values, orders):
    evens = [order for order in orders if order != 1]
    out = {order: TAPS[order][0] * values[REACH] for order in evens}
    for t in range(1, REACH + 1):
        if evens:
            pair = values[REACH + t] + values[REACH - t]
            for order in evens:
                out[order] = out[order] + TAPS[order][t] * pair
    if 1 in orders:
        out[1] = odd(values)
    return out


ACOS = (
    1.5707963050,
    -0.2145988016,
    0.0889789874,
    -0.0501743046,
    0.0308918810,
    -0.0170881256,
    0.0066700901,
    -0.0012624911,
)


def horner(x, coefs):
    out = coefs[-1]
    for coef in coefs[-2::-1]:
        out = out * x + coef
    return out


def vessel_grads(hxx, hyy, hzz, hxy, hxz, hyz, cot):
    limit = np.float32(0.999999)
    mean = (hxx + hyy + hzz) * (1.0 / 3.0)
    dx, dy, dz = hxx - mean, hyy - mean, hzz - mean
    xy2, xz2, yz2 = hxy * hxy, hxz * hxz, hyz * hyz
    p2 = (dx * dx + dy * dy + dz * dz + 2.0 * (xy2 + xz2 + yz2)) * (1.0 / 6.0)
    p = jnp.sqrt(p2)
    inv = lax.rsqrt(p2)
    cxx = dy * dz - yz2
    cxy = hxz * hyz - hxy * dz
    cxz = hxy * hyz - dy * hxz
    cyz = hxy * hxz - dx * hyz
    cyy = dx * dz - xz2
    czz = dx * dy - xy2
    det = dx * cxx + hxy * cxy + hxz * cxz
    raw = det / (2.0 * p * p * p)
    size = jnp.abs(raw)
    positive = raw >= 0.0
    open_ = jnp.where(size < limit, 1.0, jnp.where(size == limit, 0.5, 0.0))
    size = jnp.minimum(size, limit)
    gap = 1.0 - size
    root = gap * lax.rsqrt(gap)
    psi = root * horner(size, [c / 3.0 for c in ACOS])
    sq = psi * psi
    cos = horner(sq, [1.0, -1.0 / 2, 1.0 / 24, -1.0 / 720, 1.0 / 40320])
    sin = psi * horner(sq, [1.0, -1.0 / 6, 1.0 / 120, -1.0 / 5040])
    wide = math.sqrt(3.0) * sin
    large, side = 2.0 * cos, cos + wide
    up = jnp.where(positive, large, side)
    low = jnp.where(positive, side, large)
    mid = low - up
    upper, lower, middle = mean + p * up, mean - p * low, mean + p * mid

    u2, m2, l2 = upper * upper, middle * middle, lower * lower
    ia = 1.0 / (l2 + 1.0)
    ra = m2 * ia
    w = lax.rsqrt(m2 * l2 + 1.0)
    rb = u2 * w
    e1 = jnp.exp(-2.0 * ra)
    e2 = jnp.exp(-2.0 * rb) * cot
    e3 = jnp.exp(-0.5 * (u2 + m2 + l2))
    f1, f3 = 1.0 - e1, 1.0 - e3
    ga = 4.0 * ia * (e1 * e2 * f3)
    f12 = f1 * e2
    gb = 2.0 * f12 * f3
    gs = f12 * e3
    bw = gb * rb * (w * w)
    fu = upper * (gs - 2.0 * gb * w)
    fm = middle * (ga + bw * l2 + gs)
    fl = lower * (gs - ga * ra + bw * m2)
    gu, gl = fu - fm, fl - fm
    third = (fu + fm + fl) * (1.0 / 3.0)
    bent = (math.sqrt(3.0) / 2.0) * cos - 0.5 * sin
    near_sin = jnp.where(positive, sin, bent)
    far_sin = jnp.where(positive, bent, sin)
    gr = (gu * near_sin + gl * far_sin) * (open_ * lax.rsqrt(gap * (1.0 + size)))
    gp = gu * up - gl * low - 2.0 * raw * gr
    along = gp * inv * (1.0 / 6.0)
    cof = gr * (1.0 / 3.0) * (inv * inv)
    third = third + cof * p2
    twice_along, twice_cof = 2.0 * along, 2.0 * cof
    return (
        along * dx + cof * cxx + third,
        along * dy + cof * cyy + third,
        along * dz + cof * czz + third,
        twice_along * hxy + twice_cof * cxy,
        twice_along * hxz + twice_cof * cxz,
        twice_along * hyz + twice_cof * cyz,
    )


def mix(block, weights, exact):
    width = block.shape[1]
    dot = functools.partial(jnp.dot, preferred_element_type=jnp.float32)
    high = block.astype(jnp.bfloat16)
    rest = block - high.astype(jnp.float32)
    low = rest.astype(jnp.bfloat16)
    out = dot(jnp.concatenate([high, low], axis=1), weights[:, : 2 * width])
    out, small = out[:, :width], out[:, width:]
    if exact:
        last = (rest - low.astype(jnp.float32)).astype(jnp.bfloat16)
        small = small + dot(jnp.concatenate([high, last], axis=1), weights[:, 2 * width :])
    return out + small


def kernel(
    ny, nz, vol, cot, weights, plane_weights, out, ext, smooth, hess, back, groups, edge,
    row_in, plane_in, corner_in, send1, recv1, send2, recv2,
):
    rows, planes, width = vol.shape
    tall = rows + 2 * REACH
    deep = planes + 2 * PAD
    gy, gz = lax.axis_index("gy"), lax.axis_index("gz")

    def has(dy, dz):
        ok = None
        for step, at, count in ((dy, gy, ny), (dz, gz, nz)):
            if step:
                one = (at > 0) if step < 0 else (at < count - 1)
                ok = one if ok is None else jnp.logical_and(ok, one)
        return ok

    ext[:REACH] = jnp.zeros((REACH, deep, width), jnp.float32)
    ext[rows + REACH :] = jnp.zeros((REACH, deep, width), jnp.float32)
    ext[REACH : rows + REACH, :PAD] = jnp.zeros((rows, PAD, width), jnp.float32)
    ext[REACH : rows + REACH, planes + PAD :] = jnp.zeros((rows, PAD, width), jnp.float32)
    row_in[...] = jnp.zeros_like(row_in)
    plane_in[...] = jnp.zeros_like(plane_in)
    corner_in[...] = jnp.zeros_like(corner_in)

    barrier = pltpu.get_barrier_semaphore()
    expected = jnp.int32(0)
    for dy, dz in SIDES:
        ok = has(dy, dz)
        expected = expected + jnp.where(ok, 1, 0)

        @pl.when(ok)
        def _(dy=dy, dz=dz):
            pl.semaphore_signal(
                barrier, inc=1, device_id=(gy + dy, gz + dz),
                device_id_type=pl.DeviceIdType.MESH,
            )

    pl.semaphore_wait(barrier, expected)

    def span(step, length, size):
        if step == 0:
            return pl.ds(0, length), pl.ds(size, length)
        if step > 0:
            return pl.ds(length - size, size), pl.ds(0, size)
        return pl.ds(0, size), pl.ds(length + size, size)

    def first(side, dy, dz):
        from_rows, to_rows = span(dy, rows, REACH)
        from_planes, to_planes = span(dz, planes, PAD)
        return pltpu.make_async_remote_copy(
            src_ref=vol.at[from_rows, from_planes, :],
            dst_ref=ext.at[to_rows, to_planes, :],
            send_sem=send1.at[side], recv_sem=recv1.at[side],
            device_id=(gy + dy, gz + dz), device_id_type=pl.DeviceIdType.MESH,
        )

    for side, (dy, dz) in enumerate(SIDES):
        @pl.when(has(dy, dz))
        def _(side=side, dy=dy, dz=dz):
            first(side, dy, dz).start()

    @pl.loop(0, rows)
    def _(r):
        ext[r + REACH, PAD : planes + PAD] = vol[r]

    for member in range(6):
        @pl.loop(0, 2 * REACH)
        def _(r):
            zero = jnp.zeros((planes, width), jnp.float32)
            back[member, r] = zero
            back[member, r + rows + 2 * REACH] = zero

    def opposite(side):
        return len(SIDES) - 1 - side

    for side, (dy, dz) in enumerate(SIDES):
        @pl.when(has(dy, dz))
        def _(side=side, dy=dy, dz=dz):
            first(side, dy, dz).wait_send()

        @pl.when(has(dy, dz))
        def _(side=side, dy=dy, dz=dz):
            back_side = opposite(side)
            first(back_side, -dy, -dz).wait_recv()

    @pl.loop(0, tall)
    def _(r):
        for c in range(0, planes, 16):
            start = c + PAD - REACH
            window = [ext[r, start + t : start + t + 16] for t in range(2 * REACH + 1)]
            done = passes(window, (0, 1, 2))
            for order in range(3):
                smooth[order, r, c : c + 16] = done[order]

    @pl.loop(0, rows // 4)
    def _(block):
        @pl.loop(0, planes // 8)
        def _(c):
            base = block * 4
            at = pl.ds(pl.multiple_of(c * 8, 8), 8)
            for order, todo in ((0, {0: 0, 2: 1, 1: 3}), (1, {0: 4, 1: 5}), (2, {0: 2})):
                held = [smooth[order, base + t, at] for t in range(2 * REACH + 4)]
                for r in range(4):
                    done = passes(held[r : r + 2 * REACH + 1], tuple(todo))
                    for y_order, member in todo.items():
                        hess[member, base + r, at] = done[y_order]

    @pl.loop(0, rows // 4)
    def _(block):
        at = pl.ds(block * 4, 4)
        for member in range(6):
            field = hess[member, at].reshape(4 * planes, width)
            field = mix(field, weights[X_ORDERS[member]], True)
            hess[member, at] = field.reshape(4, planes, width)

    @pl.loop(0, rows)
    def _(r):
        @pl.loop(0, planes // 16)
        def _(c):
            at = pl.ds(pl.multiple_of(c * 16, 16), 16)
            grads = vessel_grads(*[hess[m, r, at] for m in range(6)], cot[r, at])
            for member in range(6):
                hess[member, r, at] = grads[member]

    @pl.loop(0, rows // 4)
    def _(block):
        for member in range(6):
            field = hess[member, pl.ds(block * 4, 4)].reshape(4 * planes, width)
            field = mix(field, weights[3 + X_ORDERS[member]], False)
            back[member, pl.ds(block * 4 + 2 * REACH, 4)] = field.reshape(4, planes, width)

    def landing(dy, dz):
        if dy and dz:
            return corner_in.at[(dy + 1) // 2, (dz + 1) // 2]
        if dy:
            return row_in.at[(dy + 1) // 2]
        return plane_in.at[(dz + 1) // 2]

    def taken(step, length, size):
        if step == 0:
            return pl.ds(size, length)
        return pl.ds(length + size, size) if step > 0 else pl.ds(0, size)

    def second(side, dy, dz):
        return pltpu.make_async_remote_copy(
            src_ref=edge.at[taken(dy, rows, REACH), taken(dz, planes, PAD), :],
            dst_ref=landing(dy, dz),
            send_sem=send2.at[side], recv_sem=recv2.at[side],
            device_id=(gy + dy, gz + dz), device_id_type=pl.DeviceIdType.MESH,
        )

    def row_block(block):
        @pl.loop(0, planes // 8)
        def _(c):
            base = block * 4
            at = pl.ds(pl.multiple_of(c * 8, 8), 8)

            def held(member):
                return [back[member, base + t, at] for t in range(2 * REACH + 4)]

            for group, terms in (
                (0, ((0, 0), (1, 2), (3, 1))),
                (1, ((4, 0), (5, 1))),
                (2, ((2, 0),)),
            ):
                total = [None] * 4
                for member, order in terms:
                    values = held(member)
                    for r in range(4):
                        window = values[r : r + 2 * REACH + 1]
                        if order == 1:
                            total[r] = total[r] - odd(window)
                        elif total[r] is None:
                            total[r] = even(window, order)
                        else:
                            total[r] = total[r] + even(window, order)
                for r in range(4):
                    groups[base + r, pl.ds(pl.multiple_of(group * planes + c * 8, 8), 8)] = total[r]

        for n in range(4):
            r = block * 4 + n
            field = groups[r]
            high = field.astype(jnp.bfloat16)
            low = (field - high.astype(jnp.float32)).astype(jnp.bfloat16)
            both = jnp.concatenate([high, low], axis=1)
            done = jnp.dot(plane_weights[...], both, preferred_element_type=jnp.float32)
            edge[r] = done[:deep, :width] + done[:deep, width:] + done[deep:, :width]

    def send(wanted):
        for side, (dy, dz) in enumerate(SIDES):
            if wanted(dy):
                @pl.when(has(dy, dz))
                def _(side=side, dy=dy, dz=dz):
                    second(side, dy, dz).start()

    outer = -(-REACH // 4)
    blocks = tall // 4
    for block in [*range(outer), *range(blocks - outer, blocks)]:
        row_block(block)
    send(lambda dy: dy != 0)
    pl.loop(outer, blocks - outer)(row_block)
    send(lambda dy: dy == 0)

    @pl.loop(0, rows)
    def _(r):
        out[r] = edge[r + REACH, PAD : planes + PAD]

    for side, (dy, dz) in enumerate(SIDES):
        @pl.when(has(dy, dz))
        def _(side=side, dy=dy, dz=dz):
            second(side, dy, dz).wait_send()

        @pl.when(has(dy, dz))
        def _(side=side, dy=dy, dz=dz):
            second(opposite(side), -dy, -dz).wait_recv()

    for y, at_rows in ((1, slice(0, REACH)), (0, slice(rows - REACH, rows))):
        out[at_rows] = out[at_rows] + row_in[y]
    for z, at_planes in ((1, slice(0, PAD)), (0, slice(planes - PAD, planes))):
        out[:, at_planes] = out[:, at_planes] + plane_in[z]
        for y, at_rows in ((1, slice(0, REACH)), (0, slice(rows - REACH, rows))):
            out[at_rows, at_planes] = out[at_rows, at_planes] + corner_in[y, z]


def solution(mesh):
    ny, nz = mesh.shape["gy"], mesh.shape["gz"]

    def per_device(volume, cotangent):
        rows, planes, width = volume.shape
        tall, deep = rows + 2 * REACH, planes + 2 * PAD
        whole = pl.BlockSpec(memory_space=pltpu.VMEM)
        f32 = jnp.float32
        return pl.pallas_call(
            functools.partial(kernel, ny, nz),
            out_shape=jax.ShapeDtypeStruct(volume.shape, f32),
            in_specs=[whole] * 4,
            out_specs=whole,
            scratch_shapes=[
                pltpu.VMEM((tall, deep, width), f32),
                pltpu.VMEM((3, tall, planes, width), f32),
                pltpu.VMEM((6, rows, planes, width), f32),
                pltpu.VMEM((6, rows + 4 * REACH, planes, width), f32),
                pltpu.VMEM((tall, 3 * planes, width), f32),
                pltpu.VMEM((tall, deep, width), f32),
                pltpu.VMEM((2, REACH, planes, width), f32),
                pltpu.VMEM((2, rows, PAD, width), f32),
                pltpu.VMEM((2, 2, REACH, PAD, width), f32),
                pltpu.SemaphoreType.DMA((8,)),
                pltpu.SemaphoreType.DMA((8,)),
                pltpu.SemaphoreType.DMA((8,)),
                pltpu.SemaphoreType.DMA((8,)),
            ],
            compiler_params=pltpu.CompilerParams(
                collective_id=0, has_side_effects=True, vmem_limit_bytes=56 * 2**20
            ),
        )(volume, cotangent, jnp.asarray(split_weights(width)), jnp.asarray(spread_weights(planes)))

    placed = (P("gy", "gz", None), P("gy", "gz", None))
    return jax.shard_map(
        per_device, mesh=mesh, in_specs=placed, out_specs=P("gy", "gz", None), check_vma=False
    )
```

```python
import functools
import math

import jax
import jax.numpy as jnp
import numpy as np
from jax import lax
from jax.experimental import pallas as pl
from jax.experimental.pallas import tpu as pltpu
from jax.sharding import PartitionSpec as P

REACH = 6
PAD = 8
X_ORDERS = (2, 0, 0, 1, 1, 0)
SIDES = [(dy, dz) for dy in (-1, 0, 1) for dz in (-1, 0, 1) if (dy, dz) != (0, 0)]


def kernel_taps(order):
    base = [math.exp(-t * t / 8.0) for t in range(-REACH, REACH + 1)]
    total = sum(base)
    scale = (
        lambda t: 1.0,
        lambda t: -(t / 4.0),
        lambda t: t * t / 16.0 - 0.25,
    )[order]
    return [scale(t) * base[t + REACH] / total for t in range(-REACH, REACH + 1)]


TAPS = [kernel_taps(order)[REACH:] for order in range(3)]


def split_weights(width):
    stacks = []
    for flip in (False, True):
        for order in range(3):
            taps = kernel_taps(order)
            band = np.zeros((width, width))
            for shift in range(-REACH, REACH + 1):
                band = band + taps[REACH - shift] * np.eye(width, k=shift)
            rest = 4.0 * (band.T if flip else band)
            parts = []
            for _ in range(3):
                parts.append(rest.astype(jnp.bfloat16))
                rest = rest - parts[-1].astype(np.float64)
            b1, b2, b3 = parts
            top = np.concatenate([b1, b2, b3], axis=1)
            bottom = np.concatenate([b1, b2, b1], axis=1)
            stacks.append(np.concatenate([top, bottom], axis=0))
    return np.stack(stacks)


def spread_weights(planes):
    deep = planes + 2 * PAD
    band = np.zeros((deep, 3 * planes))
    for order in range(3):
        taps = kernel_taps(order)
        for t in range(-REACH, REACH + 1):
            band[:, order * planes : (order + 1) * planes] += taps[t + REACH] * np.eye(
                deep, planes, k=-PAD - t
            )
    high = band.astype(jnp.bfloat16)
    low = (band - high.astype(np.float64)).astype(jnp.bfloat16)
    return np.concatenate([high, low], axis=0)


def even(values, order):
    taps = TAPS[order]
    out = taps[0] * values[REACH]
    for t in range(1, REACH + 1):
        out = out + taps[t] * (values[REACH + t] + values[REACH - t])
    return out


def odd(values):
    taps = TAPS[1]
    out = taps[1] * (values[REACH + 1] - values[REACH - 1])
    for t in range(2, REACH + 1):
        out = out + taps[t] * (values[REACH + t] - values[REACH - t])
    return out


def passes(values, orders):
    evens = [order for order in orders if order != 1]
    out = {order: TAPS[order][0] * values[REACH] for order in evens}
    for t in range(1, REACH + 1):
        if evens:
            pair = values[REACH + t] + values[REACH - t]
            for order in evens:
                out[order] = out[order] + TAPS[order][t] * pair
    if 1 in orders:
        out[1] = odd(values)
    return out


ACOS = (
    1.5707963050,
    -0.2145988016,
    0.0889789874,
    -0.0501743046,
    0.0308918810,
    -0.0170881256,
    0.0066700901,
    -0.0012624911,
)


def horner(x, coefs):
    out = coefs[-1]
    for coef in coefs[-2::-1]:
        out = out * x + coef
    return out


def vessel_grads(hxx, hyy, hzz, hxy, hxz, hyz, cot):
    limit = np.float32(0.999999)
    mean = (hxx + hyy + hzz) * (1.0 / 3.0)
    dx, dy, dz = hxx - mean, hyy - mean, hzz - mean
    xy2, xz2, yz2 = hxy * hxy, hxz * hxz, hyz * hyz
    p2 = (dx * dx + dy * dy + dz * dz + 2.0 * (xy2 + xz2 + yz2)) * (1.0 / 6.0)
    p = jnp.sqrt(p2)
    inv = lax.rsqrt(p2)
    cxx = dy * dz - yz2
    cxy = hxz * hyz - hxy * dz
    cxz = hxy * hyz - dy * hxz
    cyz = hxy * hxz - dx * hyz
    cyy = dx * dz - xz2
    czz = dx * dy - xy2
    det = dx * cxx + hxy * cxy + hxz * cxz
    raw = det / (2.0 * p * p * p)
    size = jnp.abs(raw)
    positive = raw >= 0.0
    open_ = jnp.where(size < limit, 1.0, jnp.where(size == limit, 0.5, 0.0))
    size = jnp.minimum(size, limit)
    gap = 1.0 - size
    root = gap * lax.rsqrt(gap)
    psi = root * horner(size, [c / 3.0 for c in ACOS])
    sq = psi * psi
    cos = horner(sq, [1.0, -1.0 / 2, 1.0 / 24, -1.0 / 720, 1.0 / 40320])
    sin = psi * horner(sq, [1.0, -1.0 / 6, 1.0 / 120, -1.0 / 5040])
    wide = math.sqrt(3.0) * sin
    large, side = 2.0 * cos, cos + wide
    up = jnp.where(positive, large, side)
    low = jnp.where(positive, side, large)
    mid = low - up
    upper, lower, middle = mean + p * up, mean - p * low, mean + p * mid

    u2, m2, l2 = upper * upper, middle * middle, lower * lower
    ia = 1.0 / (l2 + 1.0)
    ra = m2 * ia
    w = lax.rsqrt(m2 * l2 + 1.0)
    rb = u2 * w
    e1 = jnp.exp(-2.0 * ra)
    e2 = jnp.exp(-2.0 * rb) * cot
    e3 = jnp.exp(-0.5 * (u2 + m2 + l2))
    f1, f3 = 1.0 - e1, 1.0 - e3
    ga = 4.0 * ia * (e1 * e2 * f3)
    f12 = f1 * e2
    gb = 2.0 * f12 * f3
    gs = f12 * e3
    bw = gb * rb * (w * w)
    fu = upper * (gs - 2.0 * gb * w)
    fm = middle * (ga + bw * l2 + gs)
    fl = lower * (gs - ga * ra + bw * m2)
    gu, gl = fu - fm, fl - fm
    third = (fu + fm + fl) * (1.0 / 3.0)
    bent = (math.sqrt(3.0) / 2.0) * cos - 0.5 * sin
    near_sin = jnp.where(positive, sin, bent)
    far_sin = jnp.where(positive, bent, sin)
    gr = (gu * near_sin + gl * far_sin) * (open_ * lax.rsqrt(gap * (1.0 + size)))
    gp = gu * up - gl * low - 2.0 * raw * gr
    along = gp * inv * (1.0 / 6.0)
    cof = gr * (1.0 / 3.0) * (inv * inv)
    third = third + cof * p2
    twice_along, twice_cof = 2.0 * along, 2.0 * cof
    return (
        along * dx + cof * cxx + third,
        along * dy + cof * cyy + third,
        along * dz + cof * czz + third,
        twice_along * hxy + twice_cof * cxy,
        twice_along * hxz + twice_cof * cxz,
        twice_along * hyz + twice_cof * cyz,
    )


def mix(block, weights, exact):
    width = block.shape[1]
    dot = functools.partial(jnp.dot, preferred_element_type=jnp.float32)
    high = block.astype(jnp.bfloat16)
    rest = block - high.astype(jnp.float32)
    low = rest.astype(jnp.bfloat16)
    out = dot(jnp.concatenate([high, low], axis=1), weights[:, : 2 * width])
    out, small = out[:, :width], out[:, width:]
    if exact:
        last = (rest - low.astype(jnp.float32)).astype(jnp.bfloat16)
        small = small + dot(jnp.concatenate([high, last], axis=1), weights[:, 2 * width :])
    return out + small


def kernel(
    ny, nz, vol, cot, weights, plane_weights, out, ext, smooth, hess, back, groups, edge,
    row_in, plane_in, corner_in, send1, recv1, send2, recv2,
):
    rows, planes, width = vol.shape
    tall = rows + 2 * REACH
    deep = planes + 2 * PAD
    gy, gz = lax.axis_index("gy"), lax.axis_index("gz")

    def has(dy, dz):
        ok = None
        for step, at, count in ((dy, gy, ny), (dz, gz, nz)):
            if step:
                one = (at > 0) if step < 0 else (at < count - 1)
                ok = one if ok is None else jnp.logical_and(ok, one)
        return ok

    ext[:REACH] = jnp.zeros((REACH, deep, width), jnp.float32)
    ext[rows + REACH :] = jnp.zeros((REACH, deep, width), jnp.float32)
    ext[REACH : rows + REACH, :PAD] = jnp.zeros((rows, PAD, width), jnp.float32)
    ext[REACH : rows + REACH, planes + PAD :] = jnp.zeros((rows, PAD, width), jnp.float32)
    row_in[...] = jnp.zeros_like(row_in)
    plane_in[...] = jnp.zeros_like(plane_in)
    corner_in[...] = jnp.zeros_like(corner_in)

    barrier = pltpu.get_barrier_semaphore()
    expected = jnp.int32(0)
    for dy, dz in SIDES:
        ok = has(dy, dz)
        expected = expected + jnp.where(ok, 1, 0)

        @pl.when(ok)
        def _(dy=dy, dz=dz):
            pl.semaphore_signal(
                barrier, inc=1, device_id=(gy + dy, gz + dz),
                device_id_type=pl.DeviceIdType.MESH,
            )

    pl.semaphore_wait(barrier, expected)

    def span(step, length, size):
        if step == 0:
            return pl.ds(0, length), pl.ds(size, length)
        if step > 0:
            return pl.ds(length - size, size), pl.ds(0, size)
        return pl.ds(0, size), pl.ds(length + size, size)

    def first(side, dy, dz):
        from_rows, to_rows = span(dy, rows, REACH)
        from_planes, to_planes = span(dz, planes, PAD)
        return pltpu.make_async_remote_copy(
            src_ref=vol.at[from_rows, from_planes, :],
            dst_ref=ext.at[to_rows, to_planes, :],
            send_sem=send1.at[side], recv_sem=recv1.at[side],
            device_id=(gy + dy, gz + dz), device_id_type=pl.DeviceIdType.MESH,
        )

    for side, (dy, dz) in enumerate(SIDES):
        @pl.when(has(dy, dz))
        def _(side=side, dy=dy, dz=dz):
            first(side, dy, dz).start()

    @pl.loop(0, rows)
    def _(r):
        ext[r + REACH, PAD : planes + PAD] = vol[r]

    for member in range(6):
        @pl.loop(0, 2 * REACH)
        def _(r):
            zero = jnp.zeros((planes, width), jnp.float32)
            back[member, r] = zero
            back[member, r + rows + 2 * REACH] = zero

    def opposite(side):
        return len(SIDES) - 1 - side

    for side, (dy, dz) in enumerate(SIDES):
        @pl.when(has(dy, dz))
        def _(side=side, dy=dy, dz=dz):
            first(side, dy, dz).wait_send()

        @pl.when(has(dy, dz))
        def _(side=side, dy=dy, dz=dz):
            back_side = opposite(side)
            first(back_side, -dy, -dz).wait_recv()

    @pl.loop(0, tall)
    def _(r):
        for c in range(0, planes, 16):
            start = c + PAD - REACH
            window = [ext[r, start + t : start + t + 16] for t in range(2 * REACH + 1)]
            done = passes(window, (0, 1, 2))
            for order in range(3):
                smooth[order, r, c : c + 16] = done[order]

    @pl.loop(0, rows // 4)
    def _(block):
        @pl.loop(0, planes // 8)
        def _(c):
            base = block * 4
            at = pl.ds(pl.multiple_of(c * 8, 8), 8)
            for order, todo in ((0, {0: 0, 2: 1, 1: 3}), (1, {0: 4, 1: 5}), (2, {0: 2})):
                held = [smooth[order, base + t, at] for t in range(2 * REACH + 4)]
                for r in range(4):
                    done = passes(held[r : r + 2 * REACH + 1], tuple(todo))
                    for y_order, member in todo.items():
                        hess[member, base + r, at] = done[y_order]

    @pl.loop(0, rows // 4)
    def _(block):
        at = pl.ds(block * 4, 4)
        for member in range(6):
            field = hess[member, at].reshape(4 * planes, width)
            field = mix(field, weights[X_ORDERS[member]], True)
            hess[member, at] = field.reshape(4, planes, width)

    @pl.loop(0, rows)
    def _(r):
        @pl.loop(0, planes // 16, unroll=2)
        def _(c):
            at = pl.ds(pl.multiple_of(c * 16, 16), 16)
            grads = vessel_grads(*[hess[m, r, at] for m in range(6)], cot[r, at])
            for member in range(6):
                hess[member, r, at] = grads[member]

    @pl.loop(0, rows // 4)
    def _(block):
        for member in range(6):
            field = hess[member, pl.ds(block * 4, 4)].reshape(4 * planes, width)
            field = mix(field, weights[3 + X_ORDERS[member]], False)
            back[member, pl.ds(block * 4 + 2 * REACH, 4)] = field.reshape(4, planes, width)

    def landing(dy, dz):
        if dy and dz:
            return corner_in.at[(dy + 1) // 2, (dz + 1) // 2]
        if dy:
            return row_in.at[(dy + 1) // 2]
        return plane_in.at[(dz + 1) // 2]

    def taken(step, length, size):
        if step == 0:
            return pl.ds(size, length)
        return pl.ds(length + size, size) if step > 0 else pl.ds(0, size)

    def second(side, dy, dz):
        return pltpu.make_async_remote_copy(
            src_ref=edge.at[taken(dy, rows, REACH), taken(dz, planes, PAD), :],
            dst_ref=landing(dy, dz),
            send_sem=send2.at[side], recv_sem=recv2.at[side],
            device_id=(gy + dy, gz + dz), device_id_type=pl.DeviceIdType.MESH,
        )

    def row_block(block):
        @pl.loop(0, planes // 8)
        def _(c):
            base = block * 4
            at = pl.ds(pl.multiple_of(c * 8, 8), 8)

            def held(member):
                return [back[member, base + t, at] for t in range(2 * REACH + 4)]

            for group, terms in (
                (0, ((0, 0), (1, 2), (3, 1))),
                (1, ((4, 0), (5, 1))),
                (2, ((2, 0),)),
            ):
                total = [None] * 4
                for member, order in terms:
                    values = held(member)
                    for r in range(4):
                        window = values[r : r + 2 * REACH + 1]
                        if order == 1:
                            total[r] = total[r] - odd(window)
                        elif total[r] is None:
                            total[r] = even(window, order)
                        else:
                            total[r] = total[r] + even(window, order)
                for r in range(4):
                    groups[base + r, pl.ds(pl.multiple_of(group * planes + c * 8, 8), 8)] = total[r]

        for n in range(4):
            r = block * 4 + n
            field = groups[r]
            high = field.astype(jnp.bfloat16)
            low = (field - high.astype(jnp.float32)).astype(jnp.bfloat16)
            both = jnp.concatenate([high, low], axis=1)
            done = jnp.dot(plane_weights[...], both, preferred_element_type=jnp.float32)
            edge[r] = done[:deep, :width] + done[:deep, width:] + done[deep:, :width]

    def send(wanted):
        for side, (dy, dz) in enumerate(SIDES):
            if wanted(dy):
                @pl.when(has(dy, dz))
                def _(side=side, dy=dy, dz=dz):
                    second(side, dy, dz).start()

    outer = -(-REACH // 4)
    blocks = tall // 4
    for block in [*range(outer), *range(blocks - outer, blocks)]:
        row_block(block)
    send(lambda dy: dy != 0)
    pl.loop(outer, blocks - outer)(row_block)
    send(lambda dy: dy == 0)

    @pl.loop(0, rows)
    def _(r):
        out[r] = edge[r + REACH, PAD : planes + PAD]

    for side, (dy, dz) in enumerate(SIDES):
        @pl.when(has(dy, dz))
        def _(side=side, dy=dy, dz=dz):
            second(side, dy, dz).wait_send()

        @pl.when(has(dy, dz))
        def _(side=side, dy=dy, dz=dz):
            second(opposite(side), -dy, -dz).wait_recv()

    for y, at_rows in ((1, slice(0, REACH)), (0, slice(rows - REACH, rows))):
        out[at_rows] = out[at_rows] + row_in[y]
    for z, at_planes in ((1, slice(0, PAD)), (0, slice(planes - PAD, planes))):
        out[:, at_planes] = out[:, at_planes] + plane_in[z]
        for y, at_rows in ((1, slice(0, REACH)), (0, slice(rows - REACH, rows))):
            out[at_rows, at_planes] = out[at_rows, at_planes] + corner_in[y, z]


def solution(mesh):
    ny, nz = mesh.shape["gy"], mesh.shape["gz"]

    def per_device(volume, cotangent):
        rows, planes, width = volume.shape
        tall, deep = rows + 2 * REACH, planes + 2 * PAD
        whole = pl.BlockSpec(memory_space=pltpu.VMEM)
        f32 = jnp.float32
        return pl.pallas_call(
            functools.partial(kernel, ny, nz),
            out_shape=jax.ShapeDtypeStruct(volume.shape, f32),
            in_specs=[whole] * 4,
            out_specs=whole,
            scratch_shapes=[
                pltpu.VMEM((tall, deep, width), f32),
                pltpu.VMEM((3, tall, planes, width), f32),
                pltpu.VMEM((6, rows, planes, width), f32),
                pltpu.VMEM((6, rows + 4 * REACH, planes, width), f32),
                pltpu.VMEM((tall, 3 * planes, width), f32),
                pltpu.VMEM((tall, deep, width), f32),
                pltpu.VMEM((2, REACH, planes, width), f32),
                pltpu.VMEM((2, rows, PAD, width), f32),
                pltpu.VMEM((2, 2, REACH, PAD, width), f32),
                pltpu.SemaphoreType.DMA((8,)),
                pltpu.SemaphoreType.DMA((8,)),
                pltpu.SemaphoreType.DMA((8,)),
                pltpu.SemaphoreType.DMA((8,)),
            ],
            compiler_params=pltpu.CompilerParams(
                collective_id=0, has_side_effects=True, vmem_limit_bytes=56 * 2**20
            ),
        )(volume, cotangent, jnp.asarray(split_weights(width)), jnp.asarray(spread_weights(planes)))

    placed = (P("gy", "gz", None), P("gy", "gz", None))
    return jax.shard_map(
        per_device, mesh=mesh, in_specs=placed, out_specs=P("gy", "gz", None), check_vma=False
    )
```
